32 devices in a mesh: row: 8 (over z, x), col: 4 (over y, core).
Axes of the slice: x: 2, y: 2, z: 4, core: 2. Of those that a mesh axis runs over, the one named last changes fastest.
Arguments:
- child_tiles: float32 [256, 256, 256], P(('row', 'col')), may hold values from -2 to 2
- tile_dest: int32 [256, 2], P(('row', 'col')), may hold values from 0 to 31, as said below
- tile_counts: int32 [8, 4], P('row', 'col'), may hold values from 4 to 8
- child_offsets: int32 [4], replicated, may hold values from 0 to 8
Outputs:
- r_top: float32 [1024, 8192], P(None, 'col')
The draws below stay inside these ranges and needn't reach their ends.
Inputs may be any that keep to these rules, and one draw needn't show every extreme that they name: tile_dest[t, 0] is a column tile of the front and tile_dest[t, 1] is below 7. Among the 8 slots of one count entry, at most 2 name column tiles of one block of 8 consecutive column tiles (blocks start at multiples of 8); some entry reaches 2 for some block, and some block receives 2 live slots from every entry that shares a row offset residue.
All inputs are finite; a program needn't handle non-finite values.
Results may differ from the reference program's by a relative error of at most 0.00008.
Values sent between devices are 32-bit elements; how exact they have to be, the bound alone decides.
A program may use at most 128 MiB of HBM per device.

```python
import jax
import jax.numpy as jnp
from jax import lax

NB = 256
NC = 8192
PANELS = 4
CHILDREN = 4
SLOTS = 8
CAPC = 2
COUNT_ROWS = 8
COUNT_COLS = 4
RT = 64
KB = 7
CTD = 8
TILE_SLOTS = 256


def shared_center(key):
    sub_key = jax.random.fold_in(key, 7919)
    first_key, second_key, third_key = jax.random.split(sub_key, 3)
    center_row = jax.random.randint(first_key, (), 0, COUNT_ROWS)
    center_col = jax.random.randint(second_key, (), 0, COUNT_COLS)
    offsets = jax.random.randint(third_key, (CHILDREN,), 0, COUNT_ROWS + 1)
    pick_key, other_key = jax.random.split(jax.random.fold_in(sub_key, 4409))
    top_child = jax.random.randint(pick_key, (), 0, CHILDREN)
    low_child = (top_child + 1 + jax.random.randint(other_key, (), 0, CHILDREN - 1)) % CHILDREN
    child_ids = jnp.arange(CHILDREN)
    offsets = jnp.where(child_ids == top_child, COUNT_ROWS, offsets)
    offsets = jnp.where(child_ids == low_child, 0, offsets)
    return (center_row, center_col, offsets)


def center_devices(key):
    center_row, center_col, offsets = shared_center(key)
    device_ids = jnp.arange(COUNT_ROWS * COUNT_COLS)
    row_ids = device_ids // COUNT_COLS
    col_ids = device_ids % COUNT_COLS
    child_ids = col_ids // (COUNT_COLS // CHILDREN)
    arrive_row = (offsets[child_ids] + row_ids) % COUNT_ROWS
    return (arrive_row == center_row, center_col)


def draw_child_offsets(key, part):
    center_row, center_col, offsets = shared_center(key)
    return offsets.astype(jnp.int32)


def draw_tile_counts(key, part):
    is_center, center_col = center_devices(key)
    sub_key = jax.random.fold_in(key, 31)
    counts = jax.random.randint(sub_key, (COUNT_ROWS * COUNT_COLS,), SLOTS // 2, SLOTS + 1)
    counts = jnp.where(is_center, SLOTS, counts)
    return counts.reshape(COUNT_ROWS, COUNT_COLS).astype(jnp.int32)


def draw_tile_dest(key, part):
    is_center, center_col = center_devices(key)
    total = COUNT_ROWS * COUNT_COLS
    entries = COUNT_COLS * CAPC
    device_keys = jax.random.split(jax.random.fold_in(key, 57), total)

    def one_device(device_key, center_flag):
        key_a, key_b, key_c, key_d, key_e = jax.random.split(device_key, 5)
        forced = jax.random.randint(key_a, (), 0, COUNT_COLS)
        forced = jnp.where(center_flag, center_col, forced)
        scores = jax.random.permutation(key_b, entries).astype(jnp.int32)
        owners = jnp.arange(entries, dtype=jnp.int32) // CAPC
        scores = jnp.where(owners == forced, scores - entries, scores)
        chosen = jnp.argsort(scores, stable=True)[:SLOTS]
        chosen = jax.random.permutation(key_c, chosen)
        owner_cols = chosen // CAPC
        col_tiles = owner_cols * CTD + jax.random.randint(key_d, (SLOTS,), 0, CTD)
        blocks = jax.random.randint(key_e, (SLOTS,), 0, KB)
        return jnp.stack([col_tiles, blocks], axis=1).astype(jnp.int32)
    result = jax.vmap(one_device)(device_keys, is_center)
    return result.reshape(total * SLOTS, 2)


def block_scale(stream_key, shape, cuts, low, top_value):
    loudness = 1.0
    for axis_at, blocks in cuts:
        heights = jax.random.uniform(jax.random.fold_in(jax.random.fold_in(stream_key, 6), axis_at), (blocks,), jnp.float32, low / len(cuts), top_value / len(cuts))
        loudness = loudness * jnp.repeat(jnp.exp(heights), shape[axis_at] // blocks).reshape((-1,) + (1,) * (len(shape) - 1 - axis_at))
    return loudness


def scatter_about(stream_key, shape, scale, most, pieces=(), kind=jnp.bfloat16):
    factor_of = block_scale(stream_key, shape, pieces, -0.22, 0.18) if pieces else 1.0
    values = jax.random.normal(stream_key, shape, jnp.float32) * scale * factor_of
    return jnp.minimum(jnp.maximum(values, -most), most).astype(kind)


def setup_inputs(seed: int = 0) -> dict:
    keys = jax.random.split(jax.random.key(seed), 5)
    child_tiles = scatter_about(keys[0], (TILE_SLOTS, NB, NB), 0.25, 2.0, ((0, 32),), jnp.float32)
    tile_dest = draw_tile_dest(jax.random.fold_in(keys[4], 71), 0)
    tile_counts = draw_tile_counts(jax.random.fold_in(keys[4], 71), 0)
    child_offsets = draw_child_offsets(jax.random.fold_in(keys[4], 71), 0)
    return {"child_tiles": child_tiles, "tile_dest": tile_dest, "tile_counts": tile_counts, "child_offsets": child_offsets}


def reference(child_tiles, tile_dest, tile_counts, child_offsets):
    per_child = COUNT_COLS // CHILDREN
    front = jnp.zeros((RT * NB, NC), jnp.float32)

    def place_tile(slot_index, front):
        slot_index = jnp.asarray(slot_index).astype(jnp.int32)
        device_index = slot_index // SLOTS
        slot_pos = slot_index % SLOTS
        row_pos = device_index // COUNT_COLS
        col_pos = device_index % COUNT_COLS
        is_live = slot_pos < tile_counts[row_pos, col_pos]
        child_pos = col_pos // per_child
        row_tile = child_offsets[child_pos] + row_pos + COUNT_ROWS * tile_dest[slot_index, 1]
        col_tile = tile_dest[slot_index, 0]
        start_row = (row_tile * NB).astype(jnp.int32)
        start_col = (col_tile * NB).astype(jnp.int32)
        old_tile = lax.dynamic_slice(front, (start_row, start_col), (NB, NB))
        new_tile = old_tile + jnp.where(is_live, child_tiles[slot_index], jnp.zeros_like(old_tile))
        return lax.dynamic_update_slice(front, new_tile, (start_row, start_col))
    front = lax.fori_loop(0, COUNT_ROWS * COUNT_COLS * SLOTS, place_tile, front)
    width = PANELS * NB
    leading = front[:, :width]
    gram_block = jnp.dot(leading.T.astype(jnp.float32), leading.astype(jnp.float32), precision=lax.Precision.HIGHEST, preferred_element_type=jnp.float32)
    cross_terms = jnp.dot(leading.T.astype(jnp.float32), front.astype(jnp.float32), precision=lax.Precision.HIGHEST, preferred_element_type=jnp.float32)
    lower_factor = jnp.linalg.cholesky(gram_block)
    rows_out = jax.scipy.linalg.solve_triangular(lower_factor, cross_terms, lower=True)
    upper_mask = jnp.arange(NC)[None, :] >= jnp.arange(width)[:, None]
    return jnp.where(upper_mask, rows_out, jnp.zeros_like(rows_out))
```

```python
import functools

import jax
import jax.numpy as jnp
from jax import lax
from jax.experimental import pallas as pl
from jax.experimental.pallas import tpu as pltpu
from jax.sharding import PartitionSpec as P

NC = 8192
PANELS = 4
CHILDREN = 4
CAPC = 2
MAIN = 5
HELD = 64
BLK = 128
PIV = 8
STEP = 4
LANES = 128

HIGHEST = lax.Precision.HIGHEST
MESH = pl.DeviceIdType.MESH
ANY = pl.BlockSpec(memory_space=pl.ANY)
VMEM = pl.BlockSpec(memory_space=pltpu.VMEM)
SMEM = pl.BlockSpec(memory_space=pltpu.SMEM)
DMA = pltpu.SemaphoreType.DMA


def ring_row(p, nr):
    b = p // (nr // 2)
    return (1 - b) * 2 * p + b * (2 * (nr - 1 - p) + 1)


def ring_pos(r, nr):
    b = r % 2
    return (1 - b) * (r // 2) + b * (nr - 1 - r // 2)


def pack_kernel(tiles_col, dest, counts, tiles, packed, meta, buf, held, place, sem_in, sem_out):
    slots = tiles.shape[0]
    live_count = counts[0, 0]
    for s in range(slots):
        pltpu.make_async_copy(tiles.at[s], buf.at[s], sem_in.at[s]).start()
    for c in range(held.shape[0]):
        held[c] = 0
    sub = lax.broadcasted_iota(jnp.int32, meta.shape, 0)
    lane = lax.broadcasted_iota(jnp.int32, meta.shape, 1)
    table = jnp.full(meta.shape, -1, jnp.int32)
    for s in range(slots):
        live = s < live_count
        col = jnp.where(live, dest[s, 0], -1)
        owner = jnp.where(live, dest[s, 0], 0) // tiles_col
        rank = held[owner]
        held[owner] = rank + live.astype(jnp.int32)
        place[s] = jnp.where(live, owner * CAPC + rank, -1)
        table = jnp.where((sub == 0) & (lane == s), col, table)
        table = jnp.where((sub == 1) & (lane == s), dest[s, 1], table)
    meta[...] = table
    for s in range(slots):
        pltpu.make_async_copy(tiles.at[s], buf.at[s], sem_in.at[s]).wait()

        @pl.when(place[s] >= 0)
        def _():
            pltpu.make_async_copy(buf.at[s], packed.at[place[s]], sem_out.at[s]).start()
    for s in range(slots):
        @pl.when(place[s] >= 0)
        def _():
            pltpu.make_async_copy(buf.at[s], packed.at[place[s]], sem_out.at[s]).wait()


def pack(tiles, dest, counts, nc):
    slots, nb = tiles.shape[0], tiles.shape[1]
    return pl.pallas_call(
        functools.partial(pack_kernel, NC // nc // nb),
        out_shape=(
            jax.ShapeDtypeStruct((nc * CAPC, nb, nb), jnp.float32),
            jax.ShapeDtypeStruct((8, LANES), jnp.int32),
        ),
        in_specs=[SMEM, SMEM, ANY],
        out_specs=(ANY, VMEM),
        scratch_shapes=[
            pltpu.VMEM((slots, nb, nb), jnp.float32),
            pltpu.SMEM((nc,), jnp.int32),
            pltpu.SMEM((slots,), jnp.int32),
            DMA((slots,)),
            DMA((slots,)),
        ],
    )(dest, counts, tiles)


def exchange_kernel(
    nr, nc, packed, meta, leads, fronts, metas, own,
    own_in, own_out, col_send, col_recv, mate_send, mate_recv, pass_send, pass_recv,
    meta_send, meta_recv, front_send, front_recv, ring_send, ring_recv,
    half_send, half_recv, info_send, info_recv,
):
    nb = packed.shape[-1]
    row = lax.axis_index("row")
    col = lax.axis_index("col")
    core = col % 2
    plane = col // 2
    planes = nc // 2
    mate = col + 1 - 2 * core
    pos = ring_pos(row, nr)
    right = ring_row((pos + 1) % nr, nr)
    left = ring_row((pos + nr - 1) % nr, nr)
    hops = nr // 2

    barrier = pltpu.get_barrier_semaphore()
    for peer in (left, right):
        pl.semaphore_signal(barrier, inc=1, device_id=(peer, col), device_id_type=MESH)
    for d in range(1, nc):
        pl.semaphore_signal(barrier, inc=1, device_id=(row, (col + d) % nc), device_id_type=MESH)
    pl.semaphore_wait(barrier, nc + 1)

    def remote(src, dst, send, recv, to_row, to_col):
        return pltpu.make_async_remote_copy(
            src_ref=src, dst_ref=dst, send_sem=send, recv_sem=recv,
            device_id=(to_row, to_col), device_id_type=MESH,
        )

    sent = []

    def go(copy):
        copy.start()
        sent.append(copy)

    mine = packed.at[0]
    for d in range(1, planes):
        to = ((plane + d) % planes) * 2 + core
        go(remote(mine, leads.at[row, col], col_send.at[d - 1], col_recv.at[d - 1], row, to))
    go(remote(mine, leads.at[row, col], mate_send, mate_recv, row, mate))
    for d in range(1, nc):
        to = (col + d) % nc
        go(remote(meta, metas.at[row, col], meta_send.at[d - 1], meta_recv.at[d - 1], row, to))

    taken = [
        (mine, own.at[0], leads.at[row, col]),
        (packed.at[col], own.at[1], fronts.at[col]),
    ]
    for i, (src, mid, dst) in enumerate(taken):
        pltpu.make_async_copy(src, mid, own_in.at[i]).start()
    keep = pltpu.make_async_copy(meta, metas.at[row, col], own_in.at[2])
    keep.start()
    for i, (src, mid, dst) in enumerate(taken):
        pltpu.make_async_copy(src, mid, own_in.at[i]).wait()
        pltpu.make_async_copy(mid, dst, own_out.at[i]).start()

    def arrived(slot, sem):
        remote(slot, slot, mate_send, sem, row, mate).wait_recv()

    for d in range(1, planes):
        origin = ((plane + planes - d) % planes) * 2 + core
        arrived(leads.at[row, origin], col_recv.at[d - 1])
        go(remote(
            leads.at[row, origin], leads.at[row, origin],
            pass_send.at[d - 1], pass_recv.at[d - 1], row, mate,
        ))
    keep.wait()
    for i, (src, mid, dst) in enumerate(taken):
        pltpu.make_async_copy(mid, dst, own_out.at[i]).wait()
    arrived(leads.at[row, mate], mate_recv)
    for d in range(1, planes):
        origin = ((plane + planes - d) % planes) * 2 + 1 - core
        arrived(leads.at[row, origin], pass_recv.at[d - 1])
    for d in range(1, nc):
        arrived(metas.at[row, (col + nc - d) % nc], meta_recv.at[d - 1])

    half, quarter = nb // 2, nb // 4

    def part(origin, direction, step, which):
        if step < hops:
            start, size = which * half, half
        else:
            start, size = which * half + direction * quarter, quarter
        return leads.at[origin, :, :, pl.ds(pl.multiple_of(start, quarter), size), :]

    def source(direction, step):
        shift = nr - step if direction == 0 else step
        return ring_row((pos + shift) % nr, nr)

    for step in range(1, hops + 1):
        for direction, to in ((0, right), (1, left)):
            origin = source(direction, step - 1)
            block = part(origin, direction, step, core)
            go(remote(
                block, block, ring_send.at[direction, step - 1], ring_recv.at[direction, step - 1],
                to, col,
            ))
            if step < hops or direction == 0:
                info = metas.at[origin]
                go(remote(
                    info, info, info_send.at[direction, step - 1], info_recv.at[direction, step - 1],
                    to, col,
                ))
        if step == 1:
            for d in range(1, nc):
                to = (col + d) % nc
                go(remote(
                    packed.at[to], fronts.at[col], front_send.at[d - 1], front_recv.at[d - 1], row, to
                ))
        for direction in (0, 1):
            origin = source(direction, step)
            block = part(origin, direction, step, core)
            arrived(block, ring_recv.at[direction, step - 1])
            if step < hops or direction == 0:
                arrived(metas.at[origin], info_recv.at[direction, step - 1])
            go(remote(
                block, block, half_send.at[direction, step - 1], half_recv.at[direction, step - 1],
                row, mate,
            ))
    for step in range(1, hops + 1):
        for direction in (0, 1):
            arrived(
                part(source(direction, step), direction, step, 1 - core),
                half_recv.at[direction, step - 1],
            )
    for d in range(1, nc):
        arrived(fronts.at[(col + nc - d) % nc], front_recv.at[d - 1])
    for copy in sent:
        copy.wait_send()


def exchange(packed, meta, nr, nc):
    nb = packed.shape[-1]
    hops = nr // 2
    planes = nc // 2
    few = max(planes - 1, 1)
    return pl.pallas_call(
        functools.partial(exchange_kernel, nr, nc),
        out_shape=(
            jax.ShapeDtypeStruct((nr, nc, CAPC, nb, nb), jnp.float32),
            jax.ShapeDtypeStruct((nc, CAPC, nb, nb), jnp.float32),
            jax.ShapeDtypeStruct((nr, nc, 8, LANES), jnp.int32),
        ),
        in_specs=[ANY, VMEM],
        out_specs=(ANY, ANY, VMEM),
        scratch_shapes=[
            pltpu.VMEM((2, CAPC, nb, nb), jnp.float32),
            DMA((3,)), DMA((2,)),
            DMA((few,)), DMA((few,)),
            DMA, DMA,
            DMA((few,)), DMA((few,)),
            DMA((nc - 1,)), DMA((nc - 1,)),
            DMA((nc - 1,)), DMA((nc - 1,)),
            DMA((2, hops)), DMA((2, hops)),
            DMA((2, hops)), DMA((2, hops)),
            DMA((2, hops)), DMA((2, hops)),
        ],
        compiler_params=pltpu.CompilerParams(collective_id=0, has_side_effects=True),
    )(packed.reshape(nc, CAPC, nb, nb), meta)


def bucket(count, key, limit, held, names, depth):
    @pl.loop(0, limit)
    def _(r):
        held[r] = 0

    @pl.loop(0, count)
    def _(p):
        r = key[p]

        @pl.when(r >= 0)
        def _():
            n = held[r]
            names[r * depth + n] = p
            held[r] = n + 1


def gram_kernel(
    depth, lr, lc, pick, leads, fronts, gram, main, rest, held, names, tiles, buf, sem, sem_in, sem_out,
):
    nb = tiles.shape[-1]
    count = leads.shape[0]
    resident = tiles.shape[0] == count
    keep = buf.shape[0]
    first = main.shape[0]

    def pull(p, slot):
        return pltpu.make_async_copy(leads.at[p], tiles.at[slot], sem.at[slot])

    def every_lead(act):
        @pl.loop(0, count)
        def _(p):
            @pl.when(lr[p] >= 0)
            def _():
                act(pull(p, p))

    def every_front(act):
        for q in range(keep):
            @pl.when(pick[q] >= 0)
            def _():
                act(q)

    def put(q):
        out = main.at[q] if q < first else rest.at[q - first]
        return pltpu.make_async_copy(buf.at[q], out, sem_out.at[q])

    def fetch(q):
        return pltpu.make_async_copy(fronts.at[pick[q]], buf.at[q], sem_in.at[q])

    def forward(q):
        fetch(q).wait()
        put(q).start()

    if resident:
        every_lead(lambda copy: copy.start())
    every_front(lambda q: fetch(q).start())
    gram[...] = jnp.zeros_like(gram)
    bucket(count, lr, held.shape[0], held, names, depth)
    every_front(forward)
    if resident:
        every_lead(lambda copy: copy.wait())

    @pl.loop(0, count)
    def _(p):
        @pl.when(lr[p] >= 0)
        def _():
            if not resident:
                pull(p, 0).start()
                pull(p, 0).wait()

            @pl.loop(0, held[lr[p]])
            def _(i):
                q = names[lr[p] * depth + i]

                @pl.when(lc[q] >= lc[p])
                def _():
                    if not resident:
                        pull(q, 1).start()
                        pull(q, 1).wait()
                    down = pl.ds(pl.multiple_of(lc[p] * nb, nb), nb)
                    across = pl.ds(pl.multiple_of(lc[q] * nb, nb), nb)
                    gram[down, across] += lax.dot_general(
                        tiles[p if resident else 0], tiles[q if resident else 1], (((0,), (0,)), ((), ())),
                        precision=HIGHEST, preferred_element_type=jnp.float32,
                    )

    every_front(lambda q: put(q).wait())


def gram_of(lr, lc, pick, leads, fronts, rows, depth, first):
    count, nb = leads.shape[0], leads.shape[1]
    width = PANELS * nb
    keep = pick.shape[0]
    cache = count if count <= HELD else 2
    return pl.pallas_call(
        functools.partial(gram_kernel, depth),
        out_shape=(
            jax.ShapeDtypeStruct((width, width), jnp.float32),
            jax.ShapeDtypeStruct((first, nb, nb), jnp.float32),
            jax.ShapeDtypeStruct((keep - first, nb, nb), jnp.float32),
        ),
        in_specs=[SMEM] * 3 + [ANY] * 2,
        out_specs=(VMEM, ANY, ANY),
        scratch_shapes=[
            pltpu.SMEM((rows,), jnp.int32),
            pltpu.SMEM((rows * depth,), jnp.int32),
            pltpu.VMEM((cache, nb, nb), jnp.float32),
            pltpu.VMEM((keep, nb, nb), jnp.float32),
            DMA((cache,)), DMA((keep,)), DMA((keep,)),
        ],
        compiler_params=pltpu.CompilerParams(vmem_limit_bytes=60 * 1024 * 1024),
    )(lr, lc, pick, leads, fronts)


def factor_kernel(nr, gram_ref, part_ref, inv_ref, all_ref, work, diag, own, own_sem, send, recv):
    n = gram_ref.shape[0]
    blocks = n // BLK
    row = lax.axis_index("row")
    col = lax.axis_index("col")
    pos = ring_pos(row, nr)
    right = ring_row((pos + 1) % nr, nr)
    left = ring_row((pos + nr - 1) % nr, nr)
    half = part_ref.shape[1] // 2
    barrier = pltpu.get_barrier_semaphore()
    for peer in (left, right):
        pl.semaphore_signal(barrier, inc=1, device_id=(peer, col), device_id_type=MESH)
    pl.semaphore_wait(barrier, 2)

    def hop(direction, step, own_block):
        origin = ring_row((pos + (nr - step if direction == 0 else step)) % nr, nr)
        rows = pl.ds(direction * half, half)
        block = all_ref.at[origin, :, rows, :]
        return pltpu.make_async_remote_copy(
            src_ref=part_ref.at[:, rows, :] if own_block else block, dst_ref=block,
            send_sem=send.at[direction, step], recv_sem=recv.at[direction, step],
            device_id=(right if direction == 0 else left, col), device_id_type=MESH,
        )

    def landed(direction, step):
        origin = ring_row((pos + (nr - step - 1 if direction == 0 else step + 1)) % nr, nr)
        block = all_ref.at[origin, :, pl.ds(direction * half, half), :]
        pltpu.make_async_remote_copy(
            src_ref=block, dst_ref=block,
            send_sem=send.at[direction, step], recv_sem=recv.at[direction, step],
            device_id=(right, col), device_id_type=MESH,
        ).wait_recv()

    for direction in (0, 1):
        hop(direction, 0, True).start()
    pltpu.make_async_copy(part_ref, own, own_sem.at[0]).start()
    pltpu.make_async_copy(part_ref, own, own_sem.at[0]).wait()
    pltpu.make_async_copy(own, all_ref.at[row], own_sem.at[1]).start()
    per_block = -(-nr // blocks)

    work[:, :n] = gram_ref[...]
    ri = lax.broadcasted_iota(jnp.int32, (n, n), 0)
    ci = lax.broadcasted_iota(jnp.int32, (n, n), 1)
    work[:, n:] = (ri == ci).astype(jnp.float32)
    eye = (
        lax.broadcasted_iota(jnp.int32, (BLK, BLK), 0)
        == lax.broadcasted_iota(jnp.int32, (BLK, BLK), 1)
    ).astype(jnp.float32)
    lane = lax.broadcasted_iota(jnp.int32, (PIV, BLK), 1)
    sub = lax.broadcasted_iota(jnp.int32, (PIV, BLK), 0)

    @pl.loop(0, blocks)
    def _(k):
        o = pl.multiple_of(k * BLK, BLK)
        for j in range(per_block):
            step = k * per_block + j

            @pl.when((step >= 1) & (step <= nr - 1))
            def _():
                for direction in (0, 1):
                    landed(direction, step - 1)

            @pl.when((step >= 1) & (step <= nr - 2))
            def _():
                for direction in (0, 1):
                    hop(direction, step, False).start()
        diag[:, :BLK] = work[pl.ds(o, BLK), pl.ds(o, BLK)]
        diag[:, BLK:] = eye

        @pl.loop(0, BLK // PIV)
        def _(g):
            q = pl.multiple_of(g * PIV, PIV)
            upper = diag[pl.ds(q, PIV), :BLK]
            right = diag[pl.ds(q, PIV), BLK:]
            corner = pltpu.roll(upper, lax.rem(BLK - q, BLK), 1)
            parts = [corner, upper, right]
            for p in range(0, PIV, STEP):
                corner = parts[0]

                def splat(x):
                    return jnp.broadcast_to(x, (PIV, BLK))

                dd = {
                    (i, j): splat(corner[p + i : p + i + 1, p + j : p + j + 1])
                    for i in range(STEP) for j in range(i + 1)
                }
                cs = [splat(corner[:, p + i : p + i + 1]) for i in range(STEP)]
                rs = [[splat(m[p + i : p + i + 1, :]) for m in parts] for i in range(STEP)]
                for e in range(STEP):
                    d = dd[e, e]
                    s = lax.rsqrt(d)
                    s = s * (1.5 - 0.5 * (d * s) * s)
                    cs[e] = cs[e] * s
                    rs[e] = [m * s for m in rs[e]]
                    low = {i: dd[i, e] * s for i in range(e + 1, STEP)}
                    for i in range(e + 1, STEP):
                        cs[i] = cs[i] - low[i] * cs[e]
                        rs[i] = [m - low[i] * w for m, w in zip(rs[i], rs[e])]
                        for j in range(e + 1, i + 1):
                            dd[i, j] = dd[i, j] - low[i] * low[j]
                for e in range(STEP):
                    below = jnp.where(sub >= p + STEP, cs[e], 0.0)
                    parts = [
                        jnp.where(sub == p + e, w, m - below * w)
                        for m, w in zip(parts, rs[e])
                    ]
            rows = jnp.concatenate(parts[1:], axis=1)
            left = jnp.where(lane >= q + PIV, rows[:, :BLK], 0.0)
            diag[...] -= lax.dot_general(
                left, rows, (((0,), (0,)), ((), ())),
                precision=HIGHEST, preferred_element_type=jnp.float32,
            )
            diag[pl.ds(q, PIV), :] = rows

        window = pl.ds(pl.multiple_of(o + BLK, BLK), n)
        panel = jnp.dot(
            diag[:, BLK:], work[pl.ds(o, BLK), window],
            precision=HIGHEST, preferred_element_type=jnp.float32,
        )
        work[pl.ds(o, BLK), window] = panel

        @pl.loop(k + 1, blocks)
        def _(i):
            t = pl.multiple_of(i * BLK, BLK)
            work[pl.ds(t, BLK), window] -= lax.dot_general(
                work[pl.ds(o, BLK), pl.ds(t, BLK)], work[pl.ds(o, BLK), window],
                (((0,), (0,)), ((), ())),
                precision=HIGHEST, preferred_element_type=jnp.float32,
            )

    inv_ref[...] = work[:, n:]
    for direction in (0, 1):
        hop(direction, 0, True).wait_send()

        @pl.loop(1, nr - 1)
        def _(step):
            hop(direction, step, False).wait_send()
    pltpu.make_async_copy(own, all_ref.at[row], own_sem.at[1]).wait()


def inverse_factor(gram, part, nr):
    n = gram.shape[0]
    return pl.pallas_call(
        functools.partial(factor_kernel, nr),
        out_shape=(
            jax.ShapeDtypeStruct((n, n), jnp.float32),
            jax.ShapeDtypeStruct((nr,) + part.shape, jnp.float32),
        ),
        in_specs=[VMEM, ANY],
        out_specs=(VMEM, ANY),
        scratch_shapes=[
            pltpu.VMEM((n, 2 * n), jnp.float32),
            pltpu.VMEM((BLK, 2 * BLK), jnp.float32),
            pltpu.VMEM(part.shape, jnp.float32),
            DMA((2,)), DMA((2, nr - 1)), DMA((2, nr - 1)),
        ],
        compiler_params=pltpu.CompilerParams(
            vmem_limit_bytes=40 * 1024 * 1024, collective_id=1, has_side_effects=True
        ),
    )(gram, part)


def ring_kernel(nr, parts, part_index, all_ref, own, own_sem, send, recv):
    row = lax.axis_index("row")
    col = lax.axis_index("col")
    pos = ring_pos(row, nr)
    right = ring_row((pos + 1) % nr, nr)
    left = ring_row((pos + nr - 1) % nr, nr)
    count = own.shape[0]
    half = own.shape[1] // 2
    mine = parts.at[pl.ds(part_index * count, count)]
    barrier = pltpu.get_barrier_semaphore()
    for peer in (left, right):
        pl.semaphore_signal(barrier, inc=1, device_id=(peer, col), device_id_type=MESH)
    pl.semaphore_wait(barrier, 2)
    take = pltpu.make_async_copy(mine, own, own_sem.at[0])
    take.start()
    take.wait()
    give = pltpu.make_async_copy(own, all_ref.at[row], own_sem.at[1])
    give.start()
    give.wait()
    sent = []
    for step in range(nr - 1):
        for direction, to in ((0, right), (1, left)):
            origin = ring_row((pos + (nr - step if direction == 0 else step)) % nr, nr)
            block = all_ref.at[origin, :, pl.ds(direction * half, half), :]
            copy = pltpu.make_async_remote_copy(
                src_ref=block, dst_ref=block,
                send_sem=send.at[direction, step], recv_sem=recv.at[direction, step],
                device_id=(to, col), device_id_type=MESH,
            )
            copy.start()
            sent.append(copy)
        for direction in (0, 1):
            origin = ring_row((pos + (nr - step - 1 if direction == 0 else step + 1)) % nr, nr)
            block = all_ref.at[origin, :, pl.ds(direction * half, half), :]
            pltpu.make_async_remote_copy(
                src_ref=block, dst_ref=block,
                send_sem=send.at[direction, step], recv_sem=recv.at[direction, step],
                device_id=(right, col), device_id_type=MESH,
            ).wait_recv()
    for copy in sent:
        copy.wait_send()


def ring(parts, index, first, nr):
    nb = parts.shape[-1]

    def kernel(*refs):
        ring_kernel(nr, refs[0], index, *refs[1:])

    return pl.pallas_call(
        kernel,
        out_shape=jax.ShapeDtypeStruct((nr, first, nb, nb), jnp.float32),
        in_specs=[ANY],
        out_specs=ANY,
        scratch_shapes=[
            pltpu.VMEM((first, nb, nb), jnp.float32),
            DMA((2,)), DMA((2, nr - 1)), DMA((2, nr - 1)),
        ],
        compiler_params=pltpu.CompilerParams(collective_id=2 + index, has_side_effects=True),
    )(parts)


def solve_kernel(depth, opening, closing, here, lr, lc, fr, fc, inverse, start, leads, fronts, out,
                 held, names, col_held, col_names, lead_tiles, front_tiles, cross, lead_sem, front_sem):
    j = pl.program_id(0)
    nb = cross.shape[1]
    lead_count, front_count = leads.shape[0], front_tiles.shape[0]
    resident = lead_tiles.shape[0] == lead_count
    tiles_col = pl.num_programs(0)

    def pull(p, slot):
        return pltpu.make_async_copy(leads.at[p], lead_tiles.at[slot], lead_sem.at[slot])

    def bring(q):
        return pltpu.make_async_copy(fronts.at[q], front_tiles.at[q], front_sem.at[q])

    def every(count, key, act):
        @pl.loop(0, count)
        def _(p):
            @pl.when(key[p] >= 0)
            def _():
                act(p)

    @pl.when(j == 0)
    def _():
        if resident:
            every(lead_count, lr, lambda p: pull(p, p).start())
        every(front_count, fr, lambda q: bring(q).start())
        bucket(lead_count, lr, held.shape[0], held, names, depth)
        bucket(front_count, fc, col_held.shape[0], col_held, col_names, front_count)
        if resident:
            every(lead_count, lr, lambda p: pull(p, p).wait())
        every(front_count, fr, lambda q: bring(q).wait())

    tile = here[0] * tiles_col + j
    if opening:
        led = tile < PANELS

        @pl.when(led)
        def _():
            cross[...] = start[:, pl.ds(pl.multiple_of(jnp.minimum(tile, PANELS - 1) * nb, nb), nb)]

        @pl.when(jnp.logical_not(led))
        def _():
            cross[...] = jnp.zeros_like(cross)
    else:
        cross[...] = start[...]

    @pl.loop(0, col_held[j])
    def _(i):
        q = col_names[j * front_count + i]
        r = fr[q]

        @pl.loop(0, held[r])
        def _(e):
            p = names[r * depth + e]
            if not resident:
                pull(p, 0).start()
                pull(p, 0).wait()
            down = pl.ds(pl.multiple_of(lc[p] * nb, nb), nb)
            cross[down, :] += lax.dot_general(
                lead_tiles[p if resident else 0], front_tiles[q], (((0,), (0,)), ((), ())),
                precision=HIGHEST, preferred_element_type=jnp.float32,
            )

    if not closing:
        out[...] = cross[...]
        return
    for i in range(PANELS):
        rows = slice(i * nb, (i + 1) * nb)
        top = jnp.dot(
            inverse[rows, : (i + 1) * nb], cross[: (i + 1) * nb, :],
            precision=HIGHEST, preferred_element_type=jnp.float32,
        )
        down = lax.broadcasted_iota(jnp.int32, (nb, nb), 0) + i * nb
        across = lax.broadcasted_iota(jnp.int32, (nb, nb), 1) + tile * nb
        out[rows, :] = jnp.where(across >= down, top, 0.0)


def solve(tables, inverse, start, leads, fronts, rows, depth, tiles_col, opening, closing):
    width = inverse.shape[0]
    nb = leads.shape[-1]
    count = leads.shape[0]
    cache = count if count <= HELD else 1
    fronts = fronts.reshape(-1, nb, nb)
    step = pl.BlockSpec((width, nb), lambda j: (0, j))
    return pl.pallas_call(
        functools.partial(solve_kernel, depth, opening, closing),
        grid=(tiles_col,),
        out_shape=jax.ShapeDtypeStruct((width, tiles_col * nb), jnp.float32),
        in_specs=[SMEM] * 5 + [VMEM, VMEM if opening else step] + [ANY] * 2,
        out_specs=step,
        scratch_shapes=[
            pltpu.SMEM((rows,), jnp.int32),
            pltpu.SMEM((rows * depth,), jnp.int32),
            pltpu.SMEM((tiles_col,), jnp.int32),
            pltpu.SMEM((tiles_col * fronts.shape[0],), jnp.int32),
            pltpu.VMEM((cache, nb, nb), jnp.float32),
            pltpu.VMEM(fronts.shape, jnp.float32),
            pltpu.VMEM((width, nb), jnp.float32),
            DMA((cache,)), DMA((fronts.shape[0],)),
        ],
        compiler_params=pltpu.CompilerParams(vmem_limit_bytes=60 * 1024 * 1024),
    )(*tables, inverse, start, leads, fronts)


def shards(child_tiles, tile_dest, tile_counts, child_offsets):
    nr = lax.axis_size("row")
    nc = lax.axis_size("col")
    row_here = lax.axis_index("row")
    col_here = lax.axis_index("col")
    slots, nb = child_tiles.shape[0], child_tiles.shape[1]
    tiles_col = NC // nc // nb
    i32 = jnp.int32

    packed, meta = pack(child_tiles, tile_dest, tile_counts, nc)
    leads, fronts, metas = exchange(packed, meta, nr, nc)

    ctile = metas[:, :, 0, :slots]
    block = metas[:, :, 1, :slots]
    offsets = jnp.repeat(child_offsets, nc // CHILDREN)
    row_tile = offsets[None, :, None] + jnp.arange(nr, dtype=i32)[:, None, None] + nr * block
    owner = jnp.where(ctile >= 0, ctile // tiles_col, -1)
    before = jnp.arange(slots)[:, None] < jnp.arange(slots)[None, :]

    def slotted(which, value):
        rank = jnp.sum((which[..., :, None] & before).astype(i32), axis=-2)
        hit = which[..., None, :] & (rank[..., None, :] == jnp.arange(CAPC)[:, None])
        return jnp.sum(jnp.where(hit, value[..., None, :] + 1, 0), axis=-1) - 1

    lead_col = slotted(owner == 0, ctile)
    lead_row = slotted(owner == 0, row_tile)
    lead_row = jnp.where((lead_col >= 0) & (lead_col < PANELS), lead_row, -1).reshape(nr * nc * CAPC)
    lead_col = lead_col.reshape(nr * nc * CAPC)

    keep = nc * CAPC
    first = min(MAIN, keep, HELD // nr)
    rounds = -(-keep // first)
    total = rounds * first

    met_all = jnp.any(row_tile[..., None] == lead_row, axis=-1) & (ctile >= PANELS)
    counts = jnp.sum(
        (met_all[..., None] & (owner[..., None] == jnp.arange(nc))).astype(i32), axis=(1, 2)
    )
    most = jnp.max(counts)

    my_col = slotted(owner == col_here, ctile).reshape(nr, keep)
    my_row = slotted(owner == col_here, row_tile).reshape(nr, keep)
    met = jnp.any(my_row[:, :, None] == lead_row[None, None, :], axis=-1)
    useful = met & (my_col >= PANELS)
    earlier = jnp.arange(keep)[:, None] < jnp.arange(keep)[None, :]
    rank = jnp.sum((useful[:, :, None] & earlier).astype(i32), axis=1)
    hit = useful[:, None, :] & (rank[:, None, :] == jnp.arange(total)[:, None])

    def compact(value):
        return jnp.sum(jnp.where(hit, value[:, None, :] + 1, 0), axis=-1) - 1

    pick = compact(jnp.broadcast_to(jnp.arange(keep, dtype=i32), (nr, keep)))
    pick = jnp.sum(jnp.where(jnp.arange(nr)[:, None] == row_here, pick, 0), axis=0)
    front_row = compact(my_row)
    front_col = compact(my_col)
    front_col = jnp.where(front_col >= 0, front_col % tiles_col, -1)

    rows = 8 * nr
    depth = nc * CAPC
    leads = leads.reshape(nr * nc * CAPC, nb, nb)
    gram, part, rest = gram_of(
        lead_row, lead_col, pick, leads, fronts.reshape(keep, nb, nb), rows, depth, first
    )
    inverse, gathered = inverse_factor(gram, part, nr)
    here = col_here.reshape(1).astype(i32)

    def tables(i):
        cut = slice(i * first, (i + 1) * first)
        return here, lead_row, lead_col, front_row[:, cut].reshape(-1), front_col[:, cut].reshape(-1)

    def once(rest):
        return solve(tables(0), inverse, gram, leads, gathered, rows, depth, tiles_col, True, True)

    def again(rest):
        cross = solve(tables(0), inverse, gram, leads, gathered, rows, depth, tiles_col, True, False)
        for i in range(1, rounds):
            more = ring(rest, i - 1, first, nr)
            cross = solve(
                tables(i), inverse, cross, leads, more, rows, depth, tiles_col, False, i == rounds - 1
            )
        return cross

    if rounds == 1:
        return once(rest)
    return lax.cond(most <= first, once, again, rest)


def solution(mesh):
    return jax.shard_map(
        shards,
        mesh=mesh,
        in_specs=(P(("row", "col"), None, None), P(("row", "col"), None), P("row", "col"), P()),
        out_specs=P(None, "col"),
        check_vma=False,
    )
```
